32 devices in a mesh: dp: 2 (over y), slab: 16 (over z, x, core).
Axes of the slice: x: 2, y: 2, z: 4, core: 2. Of those that a mesh axis runs over, the one named last changes fastest.
Arguments:
- profiles: float32 [2, 4, 128, 128, 128], P('dp', None, 'slab'), may hold values from -4.5 to 4.5, as said below
- target_fields: float32 [2, 2, 128, 128, 128], P('dp', None, 'slab'), may hold values from -6 to 6
- lift_weight: float32 [4, 32], replicated, may hold values from -3 to 3
- local_weight: bfloat16 [32, 32], replicated, may hold values from -1 to 1
- local_bias: float32 [32], replicated, may hold values from -4 to 4
- output_weight: bfloat16 [32, 2], replicated, may hold values from -1 to 1
- output_bias: float32 [2], replicated, may hold values from -4 to 4
- mode_weight: float32 [2, 16, 16, 16, 1024], P(None, 'slab'), may hold values from -6 to 6
Outputs:
- predicted: float32 [2, 2, 128, 128, 128], P('dp', None, 'slab')
- mode_gradient: float32 [2, 16, 16, 16, 1024], P(None, 'slab', 'dp')
The draws below stay inside these ranges and needn't reach their ends.
Inputs may be any that keep to these rules, and one draw needn't show every extreme that they name: `profiles`: each input channel of each sample has zero mean over the grid, up to float32 rounding.
All inputs are finite; a program needn't handle non-finite values.
Results may differ from the reference program's by a relative error of at most 0.0061.
Values sent between devices are 32-bit elements; how exact they have to be, the bound alone decides.
A program may use at most 128 MiB of HBM per device.

```python
import jax
import jax.numpy as jnp
from jax import lax

C = 32
NIN = 4
NX = 128
NY = 128
NZ = 128
KX = 16
KY = 16
KZ = 16
SAMPLES = 2


def draw_profiles(key, part):
    shape = (SAMPLES, NIN, NX, NY, NZ)
    values = jnp.clip(jax.random.normal(key, shape, jnp.float32), -4.0, 4.0)
    return values - jnp.mean(values, axis=(2, 3, 4), keepdims=True)


def block_levels(rng, dims, cuts, smallest, largest):
    def one(position, blocks):
        draws = jax.random.uniform(jax.random.fold_in(jax.random.fold_in(rng, 6), position), (blocks,), jnp.float32, smallest / len(cuts), largest / len(cuts))
        return jnp.repeat(jnp.exp(draws), dims[position] // blocks).reshape((-1,) + (1,) * (len(dims) - position - 1))

    loudness = one(*cuts[0])
    for cut in cuts[1:]:
        loudness = loudness * one(*cut)
    return loudness


def centred(stream_key, shape, deviation, bound, pieces=(), kind=jnp.bfloat16):
    entries = jax.random.normal(stream_key, shape, jnp.float32) * deviation
    if len(pieces) > 0:
        entries = block_levels(stream_key, shape, pieces, -0.22, 0.18) * entries
    return jnp.clip(entries, min=-bound, max=bound).astype(kind)


def setup_inputs(seed: int = 0) -> dict:
    arg_keys = jax.random.split(jax.random.key(seed), 9)
    profiles = draw_profiles(jax.random.fold_in(arg_keys[8], 71), 0)
    target_fields = centred(arg_keys[1], (SAMPLES, 2, NX, NY, NZ), 1.0, 6.0, ((0, 2), (2, 16)), jnp.float32)
    lift_weight = centred(arg_keys[2], (NIN, C), NIN ** -0.5, 3.0, (), jnp.float32)
    local_weight = centred(arg_keys[3], (C, C), C ** -0.5, 1.0)
    local_bias = centred(arg_keys[4], (C,), 1.0, 4.0, (), jnp.float32)
    output_weight = centred(arg_keys[5], (C, 2), C ** -0.5, 1.0)
    output_bias = centred(arg_keys[6], (2,), 1.0, 4.0, (), jnp.float32)
    mode_weight = centred(arg_keys[7], (2, KY, KX, KZ, C * C), 1.0, 6.0, ((1, 16),), jnp.float32)
    return {"profiles": profiles, "target_fields": target_fields, "lift_weight": lift_weight, "local_weight": local_weight, "local_bias": local_bias, "output_weight": output_weight, "output_bias": output_bias, "mode_weight": mode_weight}


def mode_freqs(count):
    index_list = jnp.arange(count, dtype=jnp.int32)
    return jnp.where(index_list < count // 2, index_list, index_list - count).astype(jnp.int32)

def reference(profiles, target_fields, lift_weight, local_weight, local_bias, output_weight, output_bias, mode_weight):
    highest = lax.Precision.HIGHEST
    channels = lift_weight.shape[1]
    x_modes = jnp.mod(mode_freqs(KX), NX).astype(jnp.int32)
    y_modes = jnp.mod(mode_freqs(KY), NY).astype(jnp.int32)
    weights = mode_weight.reshape(2, KY, KX, KZ, channels, channels)
    w_complex = weights[0] + 1j * weights[1]
    doubling = jnp.where(jnp.arange(KZ) == 0, 1.0, 2.0).astype(jnp.float32)

    def retained(field):
        full_spectrum = jnp.fft.rfftn(field, axes=(1, 2, 3), norm='ortho')
        return (full_spectrum[:, x_modes][:, :, y_modes][:, :, :, :KZ], full_spectrum)

    def one_sample(running, inputs):
        sample, target = inputs
        lifted = jnp.einsum('ic,ixyz->cxyz', lift_weight, sample, precision=highest).astype(jnp.bfloat16)
        spectra, full_spectrum = retained(lifted.astype(jnp.float32))
        mixed = jnp.einsum('cpqk,qpkco->opqk', spectra, w_complex, precision=highest)
        placed = jnp.zeros(full_spectrum.shape, full_spectrum.dtype).at[:, x_modes[:, None], y_modes[None, :], :KZ].set(mixed)
        spectral = jnp.fft.irfftn(placed, s=(NX, NY, NZ), axes=(1, 2, 3), norm='ortho')
        columns = lifted.reshape(channels, -1)
        pre_act = spectral.reshape(channels, -1) + jnp.dot(local_weight.T, columns, preferred_element_type=jnp.float32) + local_bias[:, None]
        activated, slope_fn = jax.vjp(lambda value: jax.nn.gelu(value, approximate=True), pre_act)
        hidden = activated.astype(jnp.bfloat16)
        predicted = jnp.dot(output_weight.T, hidden, preferred_element_type=jnp.float32) + output_bias[:, None]
        misfit = predicted - target.reshape(2, -1)
        out_weights = output_weight.astype(jnp.float32)
        hidden_grad = out_weights[:, 0:1] * misfit[0:1] + out_weights[:, 1:2] * misfit[1:2]
        pre_grad, = slope_fn(hidden_grad)
        grad_spectra, unused_full = retained(pre_grad.reshape(channels, NX, NY, NZ))
        grad_spectra = grad_spectra * doubling[None, None, None, :]
        sample_grad = jnp.einsum('cpqk,opqk->qpkco', jnp.conj(spectra), grad_spectra)
        stacked = jnp.stack([jnp.real(sample_grad), jnp.imag(sample_grad)]).astype(jnp.float32)
        stacked = stacked.reshape(2, KY, KX, KZ, channels * channels)
        return (running + stacked, predicted.reshape(2, NX, NY, NZ))
    initial = jnp.zeros((2, KY, KX, KZ, channels * channels), jnp.float32)
    summed, predicted = lax.scan(one_sample, initial, (profiles, target_fields))
    return (predicted, summed)
```

```python
import functools
import math

import jax
import jax.numpy as jnp
import ml_dtypes
import numpy as np
from jax import lax
from jax.experimental import pallas as pl
from jax.experimental.pallas import tpu as pltpu
from jax.sharding import PartitionSpec as P

N = 128
K = 16
C = 32
NIN = 4
MESH = pl.DeviceIdType.MESH
BF = jnp.bfloat16
F32 = jnp.float32


def halves(table):
    table = np.asarray(table, np.float32)
    high = table.astype(ml_dtypes.bfloat16)
    low = (table - high.astype(np.float32)).astype(ml_dtypes.bfloat16)
    return high, low


def tables():
    freq = np.where(np.arange(K) < K // 2, np.arange(K), np.arange(K) - K)
    cell = np.arange(N)
    signed = 2.0 * np.pi * np.mod(freq[:, None] * cell[None, :], N) / N
    plain = 2.0 * np.pi * np.mod(np.arange(K)[:, None] * cell[None, :], N) / N
    norm = 1.0 / math.sqrt(N * N * N)
    doubling = np.where(np.arange(K) == 0, 1.0, 2.0)
    fy = np.concatenate([np.cos(signed), -np.sin(signed)], axis=0)
    fy_h, fy_l = halves(fy)
    fy_pair = np.concatenate([fy_h, fy_l], axis=0)
    zc, zs = np.cos(plain).T, np.sin(plain).T

    def place(count):
        out = np.zeros((count, 2, N, 2, count, K))
        for c in range(count):
            out[c, 0, :, 0, c], out[c, 0, :, 1, c] = zc, -zs
            out[c, 1, :, 0, c], out[c, 1, :, 1, c] = zs, zc
        return out.reshape(count * 2 * N, 2 * count * K)

    back = np.zeros((2, 8, K, 8, 2, N))
    for c in range(8):
        wc, ws = doubling[:, None] * np.cos(plain), doubling[:, None] * np.sin(plain)
        back[0, c, :, c, 0], back[0, c, :, c, 1] = wc, ws
        back[1, c, :, c, 0], back[1, c, :, c, 1] = -ws, wc
    back = back.reshape(2 * 8 * K, 8 * 2 * N)
    iy_h, iy_l = halves(np.concatenate([np.cos(signed).T, -np.sin(signed).T], axis=1))
    iy = np.concatenate([iy_h, iy_h, iy_l], axis=1)
    fx = np.concatenate([np.cos(signed), -np.sin(signed)], axis=0) * norm
    ix = np.stack([np.repeat(np.cos(signed).T, K, axis=1), np.repeat(np.sin(signed).T, K, axis=1)]) * norm
    rep = np.zeros((4, C, C, K))
    for c in range(C):
        rep[0, c, c, :] = 1.0
    rep = rep.reshape(4 * C, C * K).astype(ml_dtypes.bfloat16)
    tile = np.zeros((C, K, 4, C))
    for c in range(C):
        tile[c, :, :, c] = 1.0
    tile = tile.reshape(C * K, 4 * C).astype(ml_dtypes.bfloat16)
    hit = (np.arange(N)[None, :] % K == np.arange(K)[:, None]).astype(np.float32)
    first = (np.arange(N) < N // 2).astype(np.float32)
    corner = np.zeros((K, N))
    corner[0, N // 2 : N // 2 + C] = 1.0
    owner = np.zeros((N, C, C))
    for c in range(C):
        owner[N // 2 + c, c, :] = 1.0
    owner = owner.reshape(N, C * C).astype(ml_dtypes.bfloat16)
    masks = np.stack([hit, hit * first, hit * (1 - first), np.broadcast_to(np.tile(doubling, 8), (K, N)), np.broadcast_to(1.0 - 2.0 * first, (K, N)), corner]).astype(np.float32)
    return [fy_pair, *halves(place(NIN)), *halves(place(8)), *halves(back), iy, *halves(fx), *halves(ix), rep, tile, owner, masks]


def split(value):
    high = value.astype(BF)
    return high, (value - high.astype(F32)).astype(BF)


def mm(left, right):
    return jnp.dot(left, right, preferred_element_type=F32)


def left3(value, high, low):
    a, b = split(value)
    return mm(a, high) + mm(b, high) + mm(a, low)


def right3(high, low, value):
    a, b = split(value)
    return mm(high, a) + mm(high, b) + mm(low, a)


def kernel(dp, slab, prof, targ, modes, lift_wide, lift, local, bias, outw, outb,
           fy, zp_h, zp_l, zg_h, zg_l, iz_h, iz_l, iy, fx_h, fx_l, ix_h, ix_l, rep, tile, owner, masks,
           pred, grad,
           ubuf, resid, rows_pad, sp, rp, spec, e_h, e_l, wide, s_re, s_im, mixed, sm, rm, pm, b_h, b_l,
           field, slope, acc, sg, rg, xs, rx, g_re, g_im,
           p_send, p_recv, m_send, m_recv, g_send, g_recv, x_send, x_recv):
    me = lax.axis_index("slab")
    mine = lax.axis_index("dp")
    planes = prof.shape[1]
    share = K // dp

    barrier = pltpu.get_barrier_semaphore()
    for step in range(1, slab):
        pl.semaphore_signal(barrier, inc=1, device_id={"slab": lax.rem(me + step, slab)}, device_id_type=MESH)
    for step in range(1, dp):
        pl.semaphore_signal(barrier, inc=1, device_id={"dp": lax.rem(mine + step, dp)}, device_id_type=MESH)

    def copies(source, target, send, recv, axis, here, count):
        out = []
        for step in range(1, count):
            peer = lax.rem(here + step, count)
            origin = lax.rem(here + count - step, count)
            going = pltpu.make_async_remote_copy(
                src_ref=source.at[peer], dst_ref=target.at[here], send_sem=send.at[peer], recv_sem=recv.at[here],
                device_id={axis: peer}, device_id_type=MESH)
            coming = pltpu.make_async_remote_copy(
                src_ref=source.at[peer], dst_ref=target.at[origin], send_sem=send.at[peer], recv_sem=recv.at[origin],
                device_id={axis: peer}, device_id_type=MESH)
            out.append((going, coming))
        return out

    def launch(pairs, source, target, here):
        for going, _ in pairs:
            going.start()
        target[pl.ds(here, 1)] = source[pl.ds(here, 1)]

    def finish(pairs):
        for going, coming in pairs:
            coming.wait_recv()
        for going, _ in pairs:
            going.wait_send()

    e_h[...] = owner[...]
    e_l[...] = jnp.zeros_like(e_l)
    for i in range(NIN):
        e_row = lift_wide[i : i + 1, :]
        high, low = split(jnp.broadcast_to(e_row, (K, C * C)))
        e_h[i * K : (i + 1) * K, :] = high
        e_l[i * K : (i + 1) * K, :] = low
    resid[...] = jnp.zeros_like(resid)

    @pl.loop(0, planes)
    def _(x):
        rows = pl.ds(pl.multiple_of(x * K, K), K)
        for i in range(NIN):
            high, low = split(prof[i, x])
            both = mm(fy[...], high)
            u = both[: 2 * K] + both[2 * K :] + mm(fy[: 2 * K, :], low)
            ubuf[rows, 2 * i * N : (2 * i + 1) * N] = u[:K]
            ubuf[rows, (2 * i + 1) * N : (2 * i + 2) * N] = u[K:]

        @pl.loop(0, C // 4)
        def _(group):
            totals = [resid[group * 4 + j] for j in range(4)]
            for chunk in range(4):
                ys = slice(chunk * 32, (chunk + 1) * 32)
                inputs = [prof[i, x, ys, :] for i in range(NIN)]
                for j in range(4):
                    c = group * 4 + j
                    value = lift[0, c] * inputs[0]
                    for i in range(1, NIN):
                        value = value + lift[i, c] * inputs[i]
                    lost = value.astype(BF).astype(F32) - value
                    totals[j] = totals[j] + jnp.sum(lost.reshape(4, 8, N), axis=0)
            for j in range(4):
                resid[group * 4 + j] = totals[j]

    v = left3(ubuf[:, : 2 * NIN * N], zp_h[...], zp_l[...])
    for x in range(planes):
        sp[:, x, :N] = v[x * K : (x + 1) * K, :]
    rows_pad[...] = jnp.zeros_like(rows_pad)
    rows_pad[N // 2 : N // 2 + C, :] = jnp.sum(resid[...], axis=1)
    high, low = split(rows_pad[...])
    ones = jnp.ones((planes, N), BF)
    dims = (((1,), (1,)), ((), ()))
    sums = lax.dot_general(ones, high, dims, preferred_element_type=F32)
    sums = sums + lax.dot_general(ones, low, dims, preferred_element_type=F32)
    for q in range(slab):
        sp[q, :, N:] = sums

    pl.semaphore_wait(barrier, slab + dp - 2)
    pairs = copies(sp, rp, p_send, p_recv, "slab", me, slab)
    launch(pairs, sp, rp, me)
    finish(pairs)

    y = right3(fx_h[...], fx_l[...], rp[:, :, :N].reshape(N, N))
    spec[:, :N] = y[:K] + masks[4] * pltpu.roll(y[K:], N // 2, 1)
    sums = jnp.sum(rp[:, :, N:].reshape(N, N), axis=0, keepdims=True)
    scale = jnp.where(me == 0, 1.0 / (planes * math.sqrt(N * N * N)), 0.0).astype(F32)
    spec[:, N:] = jnp.zeros((K, N), F32)
    spec[:1, N:] = sums * scale

    def expand(row_of, count):
        for p in range(count):
            row, lost = row_of(p)
            row = jnp.broadcast_to(row, (K, N))
            wide[0, p * K : (p + 1) * K, :] = row * masks[1] + jnp.broadcast_to(lost, (K, N)) * masks[5]
            wide[1, p * K : (p + 1) * K, :] = pltpu.roll(row * masks[2], N // 2, 1)
        used = count * K
        s_re[:used, :] = left3(wide[0, :used, :], e_h[...], e_l[...])
        s_im[:used, :] = left3(wide[1, :used, :], e_h[...], e_l[...])

    expand(lambda p: (spec[p : p + 1, :N], spec[p : p + 1, N:]), K)

    @pl.loop(0, K * K // 16)
    def _(block):
        rows = pl.ds(pl.multiple_of(block * 16, 16), 16)
        total_re = jnp.zeros((16, N), F32)
        total_im = jnp.zeros((16, N), F32)
        for t in range(C * C // N):
            lanes = slice(t * N, (t + 1) * N)
            a, b, c, d = s_re[rows, lanes], s_im[rows, lanes], modes[0, rows, lanes], modes[1, rows, lanes]
            total_re += a * c - b * d
            total_im += a * d + b * c
        for part, value in enumerate((total_re, total_im)):
            value = value + pltpu.roll(value, 64, 1)
            mixed[part, rows, :] = value + pltpu.roll(value, 32, 1)

    spread = []
    for part in range(2):
        high, low = split(mixed[part])
        spread.append((mm(high, rep[...]) + mm(low, rep[...])))
    for og in range(4):
        lanes = slice(og * N, (og + 1) * N)
        keep = jnp.broadcast_to(masks[0][None], (K, K, N)).reshape(K * K, N)
        re, im = spread[0][:, lanes] * keep, spread[1][:, lanes] * keep
        out_re = right3(ix_h[0], ix_l[0], re) - right3(ix_h[1], ix_l[1], im)
        out_im = right3(ix_h[0], ix_l[0], im) + right3(ix_h[1], ix_l[1], re)
        sm[:, :, 2 * og * N : (2 * og + 1) * N] = out_re.reshape(slab, planes, N)
        sm[:, :, (2 * og + 1) * N : (2 * og + 2) * N] = out_im.reshape(slab, planes, N)

    pairs = copies(sm, rm, m_send, m_recv, "slab", me, slab)
    launch(pairs, sm, rm, me)
    finish(pairs)

    for x in range(planes):
        pm[x * K : (x + 1) * K, :] = rm[:, x, :]
    for og in range(4):
        high, low = split(pm[:, og * 2 * N : (og + 1) * 2 * N])

        for t in range(8):
            lanes = slice(t * 2 * N, (t + 1) * 2 * N)
            value = mm(high, iz_h[:, lanes]) + mm(low, iz_h[:, lanes]) + mm(high, iz_l[:, lanes])
            v_h, v_l = split(value)
            b_h[og * 8 + t] = v_h
            b_l[og * 8 + t] = v_l

    c0 = math.sqrt(2.0 / math.pi)
    c1 = c0 * 0.044715

    @pl.loop(0, planes)
    def _(x):
        rows = pl.ds(pl.multiple_of(x * K, K), K)
        acc[...] = jnp.zeros_like(acc)

        @pl.loop(0, C // 2)
        def _(pair):
            blocks = []
            for half in range(2):
                o = pair * 2 + half
                h = b_h[o, rows, :]
                l = b_l[o, rows, :]
                blocks.append(jnp.concatenate([h[:, :N], h[:, N:], l[:, :N], l[:, N:], h[:, :N], h[:, N:]], axis=0))
            field[...] = mm(iy[...], jnp.concatenate(blocks, axis=1))
            for chunk in range(4):
                ys = slice(chunk * 32, (chunk + 1) * 32)
                inputs = [prof[i, x, ys, :] for i in range(NIN)]
                add0, add1 = acc[0, ys, :], acc[1, ys, :]
                for half in range(2):
                    o = pair * 2 + half
                    v = field[ys, half * N : (half + 1) * N] + bias[o]
                    for i in range(NIN):
                        v = v + local[i, o] * inputs[i]
                    sq = v * v
                    t = jnp.tanh(v * (c0 + c1 * sq))
                    up = 0.5 + 0.5 * t
                    hidden = (v * up).astype(BF).astype(F32)
                    slope[o, ys, :] = up + (0.5 * v) * (1.0 - t * t) * (c0 + (3.0 * c1) * sq)
                    add0 = add0 + outw[o, 0] * hidden
                    add1 = add1 + outw[o, 1] * hidden
                acc[0, ys, :] = add0
                acc[1, ys, :] = add1

        for j in range(2):
            value = acc[j] + outb[j]
            pred[j, x] = value
            acc[j] = value - targ[j, x]

        @pl.loop(0, C // 2)
        def _(pair):
            parts = []
            for half in range(2):
                o = pair * 2 + half
                parts.append(((outw[o, 0] * acc[0] + outw[o, 1] * acc[1]) * slope[o]).astype(BF))
            both = mm(fy[...], jnp.concatenate(parts, axis=1))
            u = both[: 2 * K] + both[2 * K :]
            at = pl.multiple_of(pair * 4 * N, 4 * N)
            for half in range(2):
                lanes = slice(half * N, (half + 1) * N)
                ubuf[rows, pl.ds(at + 2 * half * N, N)] = u[:K, lanes]
                ubuf[rows, pl.ds(at + (2 * half + 1) * N, N)] = u[K:, lanes]

    for og in range(4):
        v = left3(ubuf[:, og * 16 * N : (og + 1) * 16 * N], zg_h[...], zg_l[...])
        for x in range(planes):
            sg[:, x, og * 2 * N : (og + 1) * 2 * N] = v[x * K : (x + 1) * K, :]

    pairs = copies(sg, rg, g_send, g_recv, "slab", me, slab)
    launch(pairs, sg, rg, me)
    finish(pairs)

    y = right3(fx_h[...], fx_l[...], rg[...].reshape(N, 8 * N))
    for og in range(4):
        re, im = slice(2 * og * N, (2 * og + 1) * N), slice((2 * og + 1) * N, (2 * og + 2) * N)
        out_re = (y[:K, re] - y[K:, im]) * masks[3]
        out_im = (y[:K, im] + y[K:, re]) * masks[3]
        for d in range(dp):
            ps = slice(d * share, (d + 1) * share)
            xs[d, :, re] = out_re[ps]
            xs[d, :, im] = out_im[ps]
    for d in range(dp):
        xs[d, :, 8 * N : 10 * N] = spec[d * share : (d + 1) * share, :]

    pairs = copies(xs, rx, x_send, x_recv, "dp", mine, dp)
    launch(pairs, xs, rx, mine)
    finish(pairs)

    used = share * K
    for d in range(dp):
        expand(lambda p: (rx[d, p : p + 1, 8 * N : 9 * N], rx[d, p : p + 1, 9 * N : 10 * N]), share)
        for part, out in enumerate((g_re, g_im)):
            total = None
            for og in range(4):
                lanes = slice((2 * og + part) * N, (2 * og + part + 1) * N)
                for p in range(share):
                    row = jnp.broadcast_to(rx[d, p : p + 1, lanes], (K, N))
                    wide[0, p * K : (p + 1) * K, :] = row * masks[0]
                high, low = split(wide[0, :used, :])
                term = tile[og * N : (og + 1) * N, :]
                value = mm(high, term) + mm(low, term)
                total = value if total is None else total + value
            out[...] = total
        for t in range(C * C // N):
            lanes = slice(t * N, (t + 1) * N)
            a, b = s_re[:used, lanes], s_im[:used, lanes]
            w_re = a * g_re[...] + b * g_im[...]
            w_im = a * g_im[...] - b * g_re[...]
            if d == 0:
                grad[0, :, lanes] = w_re
                grad[1, :, lanes] = w_im
            else:
                grad[0, :, lanes] += w_re
                grad[1, :, lanes] += w_im


def body(dp, slab, consts, profiles, target_fields, lift_weight, local_weight, local_bias, output_weight, output_bias, mode_weight):
    planes = profiles.shape[2]
    share = K // dp
    local = jnp.sum(lift_weight[:, :, None] * local_weight.astype(F32)[None], axis=1)
    lift_wide = jnp.repeat(lift_weight, C, axis=1)
    vmem = pl.BlockSpec(memory_space=pltpu.VMEM)
    smem = pl.BlockSpec(memory_space=pltpu.SMEM)
    dma = pltpu.SemaphoreType.DMA
    pred, grad = pl.pallas_call(
        functools.partial(kernel, dp, slab),
        out_shape=(jax.ShapeDtypeStruct((2, planes, N, N), F32), jax.ShapeDtypeStruct((2, share * K, C * C), F32)),
        in_specs=[vmem] * 4 + [smem] * 5 + [vmem] * len(consts),
        out_specs=(vmem, vmem),
        scratch_shapes=[
            pltpu.VMEM((planes * K, C * 2 * N), F32),
            pltpu.VMEM((C, 8, N), F32),
            pltpu.VMEM((N, N), F32),
            pltpu.VMEM((slab, planes, 2 * N), F32),
            pltpu.VMEM((slab, planes, 2 * N), F32),
            pltpu.VMEM((K, 2 * N), F32),
            pltpu.VMEM((N, C * C), BF),
            pltpu.VMEM((N, C * C), BF),
            pltpu.VMEM((2, K * K, N), F32),
            pltpu.VMEM((K * K, C * C), F32),
            pltpu.VMEM((K * K, C * C), F32),
            pltpu.VMEM((2, K * K, N), F32),
            pltpu.VMEM((slab, planes, 8 * N), F32),
            pltpu.VMEM((slab, planes, 8 * N), F32),
            pltpu.VMEM((planes * K, 8 * N), F32),
            pltpu.VMEM((C, planes * K, 2 * N), BF),
            pltpu.VMEM((C, planes * K, 2 * N), BF),
            pltpu.VMEM((N, 2 * N), F32),
            pltpu.VMEM((C, N, N), F32),
            pltpu.VMEM((2, N, N), F32),
            pltpu.VMEM((slab, planes, 8 * N), F32),
            pltpu.VMEM((slab, planes, 8 * N), F32),
            pltpu.VMEM((dp, share, 10 * N), F32),
            pltpu.VMEM((dp, share, 10 * N), F32),
            pltpu.VMEM((share * K, N), F32),
            pltpu.VMEM((share * K, N), F32),
            dma((slab,)), dma((slab,)), dma((slab,)), dma((slab,)), dma((slab,)), dma((slab,)), dma((dp,)), dma((dp,)),
        ],
        compiler_params=pltpu.CompilerParams(collective_id=0, has_side_effects=True, vmem_limit_bytes=56 << 20),
    )(profiles[0], target_fields[0], mode_weight.reshape(2, K * K, C * C), lift_wide, lift_weight, local, local_bias,
      output_weight.astype(F32), output_bias, *consts)
    return pred[None], grad.reshape(2, 1, share, K, C * C)


def solution(mesh):
    consts = tables()
    in_specs = (
        P("dp", None, "slab", None, None),
        P("dp", None, "slab", None, None),
        P(),
        P(),
        P(),
        P(),
        P(),
        P(None, "slab", None, None, None),
    )
    out_specs = (P("dp", None, "slab", None, None), P(None, "slab", "dp", None, None))

    def run(*args):
        return body(mesh.shape["dp"], mesh.shape["slab"], [jnp.asarray(c) for c in consts], *args)

    return jax.shard_map(run, mesh=mesh, in_specs=in_specs, out_specs=out_specs, check_vma=False)
```

```python
import functools
import math

import jax
import jax.numpy as jnp
import ml_dtypes
import numpy as np
from jax import lax
from jax.experimental import pallas as pl
from jax.experimental.pallas import tpu as pltpu
from jax.sharding import PartitionSpec as P

N = 128
K = 16
C = 32
NIN = 4
MESH = pl.DeviceIdType.MESH
BF = jnp.bfloat16
F32 = jnp.float32


def halves(table):
    table = np.asarray(table, np.float32)
    high = table.astype(ml_dtypes.bfloat16)
    low = (table - high.astype(np.float32)).astype(ml_dtypes.bfloat16)
    return high, low


def tables():
    freq = np.where(np.arange(K) < K // 2, np.arange(K), np.arange(K) - K)
    cell = np.arange(N)
    signed = 2.0 * np.pi * np.mod(freq[:, None] * cell[None, :], N) / N
    plain = 2.0 * np.pi * np.mod(np.arange(K)[:, None] * cell[None, :], N) / N
    norm = 1.0 / math.sqrt(N * N * N)
    doubling = np.where(np.arange(K) == 0, 1.0, 2.0)
    fy = np.concatenate([np.cos(signed), -np.sin(signed)], axis=0)
    fy_h, fy_l = halves(fy)
    fy_pair = np.concatenate([fy_h, fy_l], axis=0)
    zc, zs = np.cos(plain).T, np.sin(plain).T

    def place(count):
        out = np.zeros((count, 2, N, 2, count, K))
        for c in range(count):
            out[c, 0, :, 0, c], out[c, 0, :, 1, c] = zc, -zs
            out[c, 1, :, 0, c], out[c, 1, :, 1, c] = zs, zc
        return out.reshape(count * 2 * N, 2 * count * K)

    back = np.zeros((2, 8, K, 8, 2, N))
    for c in range(8):
        wc, ws = doubling[:, None] * np.cos(plain), doubling[:, None] * np.sin(plain)
        back[0, c, :, c, 0], back[0, c, :, c, 1] = wc, ws
        back[1, c, :, c, 0], back[1, c, :, c, 1] = -ws, wc
    back = back.reshape(2 * 8 * K, 8 * 2 * N)
    iy_h, _ = halves(np.concatenate([np.cos(signed).T, -np.sin(signed).T], axis=1))
    fx = np.concatenate([np.cos(signed), -np.sin(signed)], axis=0) * norm
    ix = np.stack([np.repeat(np.cos(signed).T, K, axis=1), np.repeat(np.sin(signed).T, K, axis=1)]) * norm
    rep = np.zeros((4, C, C, K))
    for c in range(C):
        rep[0, c, c, :] = 1.0
    rep = rep.reshape(4 * C, C * K).astype(ml_dtypes.bfloat16)
    tile = np.zeros((C, K, 4, C))
    for c in range(C):
        tile[c, :, :, c] = 1.0
    tile = tile.reshape(C * K, 4 * C).astype(ml_dtypes.bfloat16)
    hit = (np.arange(N)[None, :] % K == np.arange(K)[:, None]).astype(np.float32)
    first = (np.arange(N) < N // 2).astype(np.float32)
    corner = np.zeros((K, N))
    corner[0, N // 2 : N // 2 + C] = 1.0
    owner = np.zeros((N, C, C))
    for c in range(C):
        owner[N // 2 + c, c, :] = 1.0
    owner = owner.reshape(N, C * C).astype(ml_dtypes.bfloat16)
    masks = np.stack([hit, hit * first, hit * (1 - first), np.broadcast_to(np.tile(doubling, 8), (K, N)), np.broadcast_to(1.0 - 2.0 * first, (K, N)), corner]).astype(np.float32)
    return [fy_pair, *halves(place(NIN)), halves(place(8))[0], halves(back)[0], iy_h, *halves(fx), *halves(ix), rep, tile, owner, masks]


def split(value):
    high = value.astype(BF)
    return high, (value - high.astype(F32)).astype(BF)


def mm(left, right):
    return jnp.dot(left, right, preferred_element_type=F32)


def left3(value, high, low):
    a, b = split(value)
    return mm(a, high) + mm(b, high) + mm(a, low)


def right3(high, low, value):
    a, b = split(value)
    return mm(high, a) + mm(high, b) + mm(low, a)


def kernel(dp, slab, prof, targ, modes, lift_rows, local, outw_rows, lift, bias, outb,
           fy, zp_h, zp_l, zg, iz, iy, fx_h, fx_l, ix_h, ix_l, rep, tile, owner, masks,
           pred, grad,
           ubuf, resid, rows_pad, sp, rp, spec, e_h, e_l, wide, s_re, s_im, mixed, sm, rm, pm, b_h,
           field_a, field_b, pre, mix, outw, acc, sg, rg, xs, rx, g_re, g_im,
           p_send, p_recv, m_send, m_recv, g_send, g_recv, x_send, x_recv):
    me = lax.axis_index("slab")
    mine = lax.axis_index("dp")
    planes = prof.shape[1]
    share = K // dp

    barrier = pltpu.get_barrier_semaphore()
    for step in range(1, slab):
        pl.semaphore_signal(barrier, inc=1, device_id={"slab": lax.rem(me + step, slab)}, device_id_type=MESH)
    for step in range(1, dp):
        pl.semaphore_signal(barrier, inc=1, device_id={"dp": lax.rem(mine + step, dp)}, device_id_type=MESH)

    def copies(source, target, send, recv, axis, here, count):
        out = []
        for step in range(1, count):
            peer = lax.rem(here + step, count)
            origin = lax.rem(here + count - step, count)
            going = pltpu.make_async_remote_copy(
                src_ref=source.at[peer], dst_ref=target.at[here], send_sem=send.at[peer], recv_sem=recv.at[here],
                device_id={axis: peer}, device_id_type=MESH)
            coming = pltpu.make_async_remote_copy(
                src_ref=source.at[peer], dst_ref=target.at[origin], send_sem=send.at[peer], recv_sem=recv.at[origin],
                device_id={axis: peer}, device_id_type=MESH)
            out.append((going, coming))
        return out

    def launch(pairs, source, target, here):
        for going, _ in pairs:
            going.start()
        target[pl.ds(here, 1)] = source[pl.ds(here, 1)]

    def finish(pairs):
        for going, coming in pairs:
            coming.wait_recv()
        for going, _ in pairs:
            going.wait_send()

    e_h[...] = owner[...]
    e_l[...] = jnp.zeros_like(e_l)
    eye = lax.broadcasted_iota(jnp.int32, (C, C), 0) == lax.broadcasted_iota(jnp.int32, (C, C), 1)

    def down(row):
        high, low = split(jnp.where(eye, jnp.broadcast_to(row, (C, C)), 0.0))
        ones = jnp.ones((C, N), BF)
        return mm(high, ones) + mm(low, ones)

    for i in range(NIN):
        high, low = split(jnp.broadcast_to(lift_rows[i : i + 1, :], (K, C)))
        pick = owner[N // 2 : N // 2 + C, :]
        e_h[i * K : (i + 1) * K, :] = mm(high, pick).astype(BF)
        e_l[i * K : (i + 1) * K, :] = mm(low, pick).astype(BF)
        mix[i] = down((mm(high, local[...]) + mm(low, local[...]))[:1, :])
    for j in range(2):
        outw[j] = down(outw_rows[...].astype(F32)[j : j + 1, :])
    resid[...] = jnp.zeros_like(resid)

    @pl.loop(0, planes)
    def _(x):
        rows = pl.ds(pl.multiple_of(x * K, K), K)
        for i in range(NIN):
            high, low = split(prof[i, x])
            both = mm(fy[...], high)
            u = both[: 2 * K] + both[2 * K :] + mm(fy[: 2 * K, :], low)
            ubuf[rows, 2 * i * N : (2 * i + 1) * N] = u[:K]
            ubuf[rows, (2 * i + 1) * N : (2 * i + 2) * N] = u[K:]

        @pl.loop(0, C // 4)
        def _(group):
            totals = [resid[group * 4 + j] for j in range(4)]
            for chunk in range(4):
                ys = slice(chunk * 32, (chunk + 1) * 32)
                inputs = [prof[i, x, ys, :] for i in range(NIN)]
                for j in range(4):
                    c = group * 4 + j
                    value = lift[0, c] * inputs[0]
                    for i in range(1, NIN):
                        value = value + lift[i, c] * inputs[i]
                    lost = value.astype(BF).astype(F32) - value
                    totals[j] = totals[j] + jnp.sum(lost.reshape(4, 8, N), axis=0)
            for j in range(4):
                resid[group * 4 + j] = totals[j]

    v = left3(ubuf[:, : 2 * NIN * N], zp_h[...], zp_l[...])
    for x in range(planes):
        sp[:, x, :N] = v[x * K : (x + 1) * K, :]
    rows_pad[...] = jnp.zeros_like(rows_pad)
    rows_pad[N // 2 : N // 2 + C, :] = jnp.sum(resid[...], axis=1)
    high, low = split(rows_pad[...])
    ones = jnp.ones((planes, N), BF)
    dims = (((1,), (1,)), ((), ()))
    sums = lax.dot_general(ones, high, dims, preferred_element_type=F32)
    sums = sums + lax.dot_general(ones, low, dims, preferred_element_type=F32)
    for q in range(slab):
        sp[q, :, N:] = sums

    pl.semaphore_wait(barrier, slab + dp - 2)
    pairs = copies(sp, rp, p_send, p_recv, "slab", me, slab)
    launch(pairs, sp, rp, me)
    finish(pairs)

    y = right3(fx_h[...], fx_l[...], rp[:, :, :N].reshape(N, N))
    spec[:, :N] = y[:K] + masks[4] * pltpu.roll(y[K:], N // 2, 1)
    sums = jnp.sum(rp[:, :, N:].reshape(N, N), axis=0, keepdims=True)
    scale = jnp.where(me == 0, 1.0 / (planes * math.sqrt(N * N * N)), 0.0).astype(F32)
    spec[:, N:] = jnp.zeros((K, N), F32)
    spec[:1, N:] = sums * scale

    def expand(row_of, count):
        for p in range(count):
            row, lost = row_of(p)
            row = jnp.broadcast_to(row, (K, N))
            wide[0, p * K : (p + 1) * K, :] = row * masks[1] + jnp.broadcast_to(lost, (K, N)) * masks[5]
            wide[1, p * K : (p + 1) * K, :] = pltpu.roll(row * masks[2], N // 2, 1)
        used = count * K
        s_re[:used, :] = left3(wide[0, :used, :], e_h[...], e_l[...])
        s_im[:used, :] = left3(wide[1, :used, :], e_h[...], e_l[...])

    expand(lambda p: (spec[p : p + 1, :N], spec[p : p + 1, N:]), K)

    @pl.loop(0, K * K // 16)
    def _(block):
        rows = pl.ds(pl.multiple_of(block * 16, 16), 16)
        total_re = jnp.zeros((16, N), F32)
        total_im = jnp.zeros((16, N), F32)
        for t in range(C * C // N):
            lanes = slice(t * N, (t + 1) * N)
            a, b, c, d = s_re[rows, lanes], s_im[rows, lanes], modes[0, rows, lanes], modes[1, rows, lanes]
            total_re += a * c - b * d
            total_im += a * d + b * c
        for part, value in enumerate((total_re, total_im)):
            value = value + pltpu.roll(value, 64, 1)
            mixed[part, rows, :] = value + pltpu.roll(value, 32, 1)

    spread = []
    for part in range(2):
        high, low = split(mixed[part])
        spread.append((mm(high, rep[...]) + mm(low, rep[...])))
    for og in range(4):
        lanes = slice(og * N, (og + 1) * N)
        keep = jnp.broadcast_to(masks[0][None], (K, K, N)).reshape(K * K, N)
        re, im = spread[0][:, lanes] * keep, spread[1][:, lanes] * keep
        out_re = right3(ix_h[0], ix_l[0], re) - right3(ix_h[1], ix_l[1], im)
        out_im = right3(ix_h[0], ix_l[0], im) + right3(ix_h[1], ix_l[1], re)
        sm[:, :, 2 * og * N : (2 * og + 1) * N] = out_re.reshape(slab, planes, N)
        sm[:, :, (2 * og + 1) * N : (2 * og + 2) * N] = out_im.reshape(slab, planes, N)

    pairs = copies(sm, rm, m_send, m_recv, "slab", me, slab)
    launch(pairs, sm, rm, me)

    @pl.loop(0, planes)
    def _(x):
        @pl.loop(0, C // 4)
        def _(group):
            for chunk in range(4):
                ys = slice(chunk * 32, (chunk + 1) * 32)
                inputs = [prof[i, x, ys, :] for i in range(NIN)]
                for j in range(4):
                    o = group * 4 + j
                    value = mix[0, pl.ds(o, 1), :] * inputs[0] + bias[o]
                    for i in range(1, NIN):
                        value = value + mix[i, pl.ds(o, 1), :] * inputs[i]
                    pre[x, o, ys, :] = value

    finish(pairs)

    for x in range(planes):
        pm[x * K : (x + 1) * K, :] = rm[:, x, :]
    for og in range(4):
        high = pm[:, og * 2 * N : (og + 1) * 2 * N].astype(BF)
        for t in range(8):
            b_h[og * 8 + t] = mm(high, iz[:, t * 2 * N : (t + 1) * 2 * N]).astype(BF)

    c0 = math.sqrt(2.0 / math.pi)
    c1 = c0 * 0.044715

    @pl.loop(0, planes)
    def _(x):
        rows = pl.ds(pl.multiple_of(x * K, K), K)
        acc[...] = jnp.zeros_like(acc)

        def lines(pair):
            blocks = []
            for half in range(2):
                b = b_h[pair * 2 + half, rows, :]
                blocks.append(jnp.concatenate([b[:, :N], b[:, N:]], axis=0))
            return mm(iy[...], jnp.concatenate(blocks, axis=1))

        def activate(field, pair):
            w = [[outw[j, pl.ds(pair * 2 + half, 1), :] for j in range(2)] for half in range(2)]
            for chunk in range(4):
                ys = slice(chunk * 32, (chunk + 1) * 32)
                add0, add1 = acc[0, ys, :], acc[1, ys, :]
                for half in range(2):
                    o = pair * 2 + half
                    v = field[ys, half * N : (half + 1) * N] + pre[x, o, ys, :]
                    sq = v * v
                    t = jnp.tanh(v * (c0 + c1 * sq))
                    up = 0.5 + 0.5 * t
                    hidden = (v * up).astype(BF).astype(F32)
                    pre[x, o, ys, :] = up + (0.5 * v) * (1.0 - t * t) * (c0 + (3.0 * c1) * sq)
                    add0 = add0 + w[half][0] * hidden
                    add1 = add1 + w[half][1] * hidden
                acc[0, ys, :] = add0
                acc[1, ys, :] = add1

        field_a[...] = lines(0)

        @pl.loop(0, C // 4)
        def _(turn):
            field_b[...] = lines(turn * 2 + 1)
            activate(field_a, turn * 2)
            field_a[...] = lines(jnp.minimum(turn * 2 + 2, C // 2 - 1))
            activate(field_b, turn * 2 + 1)

        for j in range(2):
            value = acc[j] + outb[j]
            pred[j, x] = value
            acc[j] = value - targ[j, x]

        @pl.loop(0, C // 8)
        def _(turn):
            for sub in range(4):
                pair = turn * 4 + sub
                parts = []
                for half in range(2):
                    o = pair * 2 + half
                    grad_o = outw[0, pl.ds(o, 1), :] * acc[0] + outw[1, pl.ds(o, 1), :] * acc[1]
                    parts.append((grad_o * pre[x, o]).astype(BF))
                u = mm(fy[: 2 * K, :], jnp.concatenate(parts, axis=1))
                at = pl.multiple_of(pair * 4 * N, 4 * N)
                for half in range(2):
                    lanes = slice(half * N, (half + 1) * N)
                    ubuf[rows, pl.ds(at + 2 * half * N, N)] = u[:K, lanes]
                    ubuf[rows, pl.ds(at + (2 * half + 1) * N, N)] = u[K:, lanes]

    for og in range(4):
        high, low = split(ubuf[:, og * 16 * N : (og + 1) * 16 * N])
        v = mm(high, zg[...]) + mm(low, zg[...])
        for x in range(planes):
            sg[:, x, og * 2 * N : (og + 1) * 2 * N] = v[x * K : (x + 1) * K, :]

    pairs = copies(sg, rg, g_send, g_recv, "slab", me, slab)
    launch(pairs, sg, rg, me)
    finish(pairs)

    y = right3(fx_h[...], fx_l[...], rg[...].reshape(N, 8 * N))
    for og in range(4):
        re, im = slice(2 * og * N, (2 * og + 1) * N), slice((2 * og + 1) * N, (2 * og + 2) * N)
        out_re = (y[:K, re] - y[K:, im]) * masks[3]
        out_im = (y[:K, im] + y[K:, re]) * masks[3]
        for d in range(dp):
            ps = slice(d * share, (d + 1) * share)
            xs[d, :, re] = out_re[ps]
            xs[d, :, im] = out_im[ps]
    for d in range(dp):
        xs[d, :, 8 * N : 10 * N] = spec[d * share : (d + 1) * share, :]

    pairs = copies(xs, rx, x_send, x_recv, "dp", mine, dp)
    launch(pairs, xs, rx, mine)
    finish(pairs)

    used = share * K
    for d in range(dp):
        expand(lambda p: (rx[d, p : p + 1, 8 * N : 9 * N], rx[d, p : p + 1, 9 * N : 10 * N]), share)
        for part, out in enumerate((g_re, g_im)):
            total = None
            for og in range(4):
                lanes = slice((2 * og + part) * N, (2 * og + part + 1) * N)
                for p in range(share):
                    row = jnp.broadcast_to(rx[d, p : p + 1, lanes], (K, N))
                    wide[0, p * K : (p + 1) * K, :] = row * masks[0]
                high, low = split(wide[0, :used, :])
                term = tile[og * N : (og + 1) * N, :]
                value = mm(high, term) + mm(low, term)
                total = value if total is None else total + value
            out[...] = total
        for t in range(C * C // N):
            lanes = slice(t * N, (t + 1) * N)
            a, b = s_re[:used, lanes], s_im[:used, lanes]
            w_re = a * g_re[...] + b * g_im[...]
            w_im = a * g_im[...] - b * g_re[...]
            if d == 0:
                grad[0, :, lanes] = w_re
                grad[1, :, lanes] = w_im
            else:
                grad[0, :, lanes] += w_re
                grad[1, :, lanes] += w_im


def body(dp, slab, consts, profiles, target_fields, lift_weight, local_weight, local_bias, output_weight, output_bias, mode_weight):
    planes = profiles.shape[2]
    share = K // dp
    vmem = pl.BlockSpec(memory_space=pltpu.VMEM)
    smem = pl.BlockSpec(memory_space=pltpu.SMEM)
    dma = pltpu.SemaphoreType.DMA
    pred, grad = pl.pallas_call(
        functools.partial(kernel, dp, slab),
        out_shape=(jax.ShapeDtypeStruct((2, planes, N, N), F32), jax.ShapeDtypeStruct((2, share * K, C * C), F32)),
        in_specs=[vmem] * 6 + [smem] * 3 + [vmem] * len(consts),
        out_specs=(vmem, vmem),
        scratch_shapes=[
            pltpu.VMEM((planes * K, C * 2 * N), F32),
            pltpu.VMEM((C, 8, N), F32),
            pltpu.VMEM((N, N), F32),
            pltpu.VMEM((slab, planes, 2 * N), F32),
            pltpu.VMEM((slab, planes, 2 * N), F32),
            pltpu.VMEM((K, 2 * N), F32),
            pltpu.VMEM((N, C * C), BF),
            pltpu.VMEM((N, C * C), BF),
            pltpu.VMEM((2, K * K, N), F32),
            pltpu.VMEM((K * K, C * C), F32),
            pltpu.VMEM((K * K, C * C), F32),
            pltpu.VMEM((2, K * K, N), F32),
            pltpu.VMEM((slab, planes, 8 * N), F32),
            pltpu.VMEM((slab, planes, 8 * N), F32),
            pltpu.VMEM((planes * K, 8 * N), F32),
            pltpu.VMEM((C, planes * K, 2 * N), BF),
            pltpu.VMEM((N, 2 * N), F32),
            pltpu.VMEM((N, 2 * N), F32),
            pltpu.VMEM((planes, C, N, N), F32),
            pltpu.VMEM((NIN, C, N), F32),
            pltpu.VMEM((2, C, N), F32),
            pltpu.VMEM((2, N, N), F32),
            pltpu.VMEM((slab, planes, 8 * N), F32),
            pltpu.VMEM((slab, planes, 8 * N), F32),
            pltpu.VMEM((dp, share, 10 * N), F32),
            pltpu.VMEM((dp, share, 10 * N), F32),
            pltpu.VMEM((share * K, N), F32),
            pltpu.VMEM((share * K, N), F32),
            dma((slab,)), dma((slab,)), dma((slab,)), dma((slab,)), dma((slab,)), dma((slab,)), dma((dp,)), dma((dp,)),
        ],
        compiler_params=pltpu.CompilerParams(collective_id=0, has_side_effects=True, vmem_limit_bytes=56 << 20),
    )(profiles[0], target_fields[0], mode_weight.reshape(2, K * K, C * C), lift_weight, local_weight,
      output_weight.T, lift_weight, local_bias, output_bias, *consts)
    return pred[None], grad.reshape(2, 1, share, K, C * C)


def solution(mesh):
    consts = tables()
    in_specs = (
        P("dp", None, "slab", None, None),
        P("dp", None, "slab", None, None),
        P(),
        P(),
        P(),
        P(),
        P(),
        P(None, "slab", None, None, None),
    )
    out_specs = (P("dp", None, "slab", None, None), P(None, "slab", "dp", None, None))

    def run(*args):
        return body(mesh.shape["dp"], mesh.shape["slab"], [jnp.asarray(c) for c in consts], *args)

    return jax.shard_map(run, mesh=mesh, in_specs=in_specs, out_specs=out_specs, check_vma=False)
```

```python
import functools
import math

import jax
import jax.numpy as jnp
import ml_dtypes
import numpy as np
from jax import lax
from jax.experimental import pallas as pl
from jax.experimental.pallas import tpu as pltpu
from jax.sharding import PartitionSpec as P

N = 128
K = 16
C = 32
NIN = 4
MESH = pl.DeviceIdType.MESH
BF = jnp.bfloat16
F32 = jnp.float32


def halves(table):
    table = np.asarray(table, np.float32)
    high = table.astype(ml_dtypes.bfloat16)
    low = (table - high.astype(np.float32)).astype(ml_dtypes.bfloat16)
    return high, low


def tables():
    freq = np.where(np.arange(K) < K // 2, np.arange(K), np.arange(K) - K)
    cell = np.arange(N)
    signed = 2.0 * np.pi * np.mod(freq[:, None] * cell[None, :], N) / N
    plain = 2.0 * np.pi * np.mod(np.arange(K)[:, None] * cell[None, :], N) / N
    norm = 1.0 / math.sqrt(N * N * N)
    doubling = np.where(np.arange(K) == 0, 1.0, 2.0)
    fy = np.concatenate([np.cos(signed), -np.sin(signed)], axis=0)
    fy_h, fy_l = halves(fy)
    fy_pair = np.concatenate([fy_h, fy_l], axis=0)
    zc, zs = np.cos(plain).T, np.sin(plain).T

    def place(count):
        out = np.zeros((count, 2, N, 2, count, K))
        for c in range(count):
            out[c, 0, :, 0, c], out[c, 0, :, 1, c] = zc, -zs
            out[c, 1, :, 0, c], out[c, 1, :, 1, c] = zs, zc
        return out.reshape(count * 2 * N, 2 * count * K)

    back = np.zeros((2, 8, K, 8, 2, N))
    for c in range(8):
        wc, ws = doubling[:, None] * np.cos(plain), doubling[:, None] * np.sin(plain)
        back[0, c, :, c, 0], back[0, c, :, c, 1] = wc, ws
        back[1, c, :, c, 0], back[1, c, :, c, 1] = -ws, wc
    back = back.reshape(2 * 8 * K, 8 * 2 * N)
    iy_h, _ = halves(np.concatenate([np.cos(signed).T, -np.sin(signed).T], axis=1))
    fx = np.concatenate([np.cos(signed), -np.sin(signed)], axis=0) * norm
    ix = np.stack([np.repeat(np.cos(signed).T, K, axis=1), np.repeat(np.sin(signed).T, K, axis=1)]) * norm
    rep = np.zeros((4, C, C, K))
    for c in range(C):
        rep[0, c, c, :] = 1.0
    rep = rep.reshape(4 * C, C * K).astype(ml_dtypes.bfloat16)
    tile = np.zeros((C, K, 4, C))
    for c in range(C):
        tile[c, :, :, c] = 1.0
    tile = tile.reshape(C * K, 4 * C).astype(ml_dtypes.bfloat16)
    hit = (np.arange(N)[None, :] % K == np.arange(K)[:, None]).astype(np.float32)
    first = (np.arange(N) < N // 2).astype(np.float32)
    corner = np.zeros((K, N))
    corner[0, N // 2 : N // 2 + C] = 1.0
    owner = np.zeros((N, C, C))
    for c in range(C):
        owner[N // 2 + c, c, :] = 1.0
    owner = owner.reshape(N, C * C).astype(ml_dtypes.bfloat16)
    masks = np.stack([hit, hit * first, hit * (1 - first), np.broadcast_to(np.tile(doubling, 8), (K, N)), np.broadcast_to(1.0 - 2.0 * first, (K, N)), corner]).astype(np.float32)
    return [fy_pair, *halves(place(NIN)), halves(place(8))[0], halves(back)[0], iy_h, *halves(fx), *halves(ix), rep, tile, owner, masks]


def split(value):
    high = value.astype(BF)
    return high, (value - high.astype(F32)).astype(BF)


def mm(left, right):
    return jnp.dot(left, right, preferred_element_type=F32)


def left3(value, high, low):
    a, b = split(value)
    return mm(a, high) + mm(b, high) + mm(a, low)


def right3(high, low, value):
    a, b = split(value)
    return mm(high, a) + mm(high, b) + mm(low, a)


def kernel(dp, slab, prof, targ, modes, lift_rows, local, outw_rows, lift, bias, outb,
           fy, zp_h, zp_l, zg, iz, iy, fx_h, fx_l, ix_h, ix_l, rep, tile, owner, masks,
           pred, grad,
           ubuf, resid, rows_pad, sp, rp, sr, rr, spec, e_h, e_l, wide, s_re, s_im, mixed, sm, rm, pm, b_h,
           field_a, field_b, pre, mix, outw, acc, sg, rg, xs, rx, g_re, g_im,
           p_send, p_recv, r_send, r_recv, m_send, m_recv, g_send, g_recv, x_send, x_recv):
    me = lax.axis_index("slab")
    mine = lax.axis_index("dp")
    planes = prof.shape[1]
    share = K // dp
    some = planes // 2

    barrier = pltpu.get_barrier_semaphore()
    for step in range(1, slab):
        pl.semaphore_signal(barrier, inc=1, device_id={"slab": lax.rem(me + step, slab)}, device_id_type=MESH)
    for step in range(1, dp):
        pl.semaphore_signal(barrier, inc=1, device_id={"dp": lax.rem(mine + step, dp)}, device_id_type=MESH)

    def copies(source, target, send, recv, axis, here, count):
        out = []
        for step in range(1, count):
            peer = lax.rem(here + step, count)
            origin = lax.rem(here + count - step, count)
            going = pltpu.make_async_remote_copy(
                src_ref=source.at[peer], dst_ref=target.at[here], send_sem=send.at[peer], recv_sem=recv.at[here],
                device_id={axis: peer}, device_id_type=MESH)
            coming = pltpu.make_async_remote_copy(
                src_ref=source.at[peer], dst_ref=target.at[origin], send_sem=send.at[peer], recv_sem=recv.at[origin],
                device_id={axis: peer}, device_id_type=MESH)
            out.append((going, coming))
        return out

    def launch(pairs, source, target, here):
        for going, _ in pairs:
            going.start()
        target[pl.ds(here, 1)] = source[pl.ds(here, 1)]

    def finish(pairs):
        for going, coming in pairs:
            coming.wait_recv()
        for going, _ in pairs:
            going.wait_send()

    e_h[...] = owner[...]
    e_l[...] = jnp.zeros_like(e_l)
    eye = lax.broadcasted_iota(jnp.int32, (C, C), 0) == lax.broadcasted_iota(jnp.int32, (C, C), 1)

    def down(row):
        high, low = split(jnp.where(eye, jnp.broadcast_to(row, (C, C)), 0.0))
        ones = jnp.ones((C, N), BF)
        return mm(high, ones) + mm(low, ones)

    for i in range(NIN):
        high, low = split(jnp.broadcast_to(lift_rows[i : i + 1, :], (K, C)))
        pick = owner[N // 2 : N // 2 + C, :]
        e_h[i * K : (i + 1) * K, :] = mm(high, pick).astype(BF)
        e_l[i * K : (i + 1) * K, :] = mm(low, pick).astype(BF)
        mix[i] = down((mm(high, local[...]) + mm(low, local[...]))[:1, :])
    for j in range(2):
        outw[j] = down(outw_rows[...].astype(F32)[j : j + 1, :])
    resid[...] = jnp.zeros_like(resid)

    @pl.loop(0, planes)
    def _(x):
        rows = pl.ds(pl.multiple_of(x * K, K), K)
        for i in range(NIN):
            high, low = split(prof[i, x])
            both = mm(fy[...], high)
            u = both[: 2 * K] + both[2 * K :] + mm(fy[: 2 * K, :], low)
            ubuf[rows, 2 * i * N : (2 * i + 1) * N] = u[:K]
            ubuf[rows, (2 * i + 1) * N : (2 * i + 2) * N] = u[K:]

    v = left3(ubuf[:, : 2 * NIN * N], zp_h[...], zp_l[...])
    for x in range(planes):
        sp[:, x, :] = v[x * K : (x + 1) * K, :]

    pl.semaphore_wait(barrier, slab + dp - 2)
    pairs = copies(sp, rp, p_send, p_recv, "slab", me, slab)
    launch(pairs, sp, rp, me)

    @pl.loop(0, planes)
    def _(x):
        @pl.loop(0, C // 4)
        def _(group):
            totals = [resid[group * 4 + j] for j in range(4)]
            for chunk in range(4):
                ys = slice(chunk * 32, (chunk + 1) * 32)
                inputs = [prof[i, x, ys, :] for i in range(NIN)]
                for j in range(4):
                    c = group * 4 + j
                    value = lift[0, c] * inputs[0]
                    for i in range(1, NIN):
                        value = value + lift[i, c] * inputs[i]
                    lost = value.astype(BF).astype(F32) - value
                    totals[j] = totals[j] + jnp.sum(lost.reshape(4, 8, N), axis=0)
            for j in range(4):
                resid[group * 4 + j] = totals[j]

    rows_pad[...] = jnp.zeros_like(rows_pad)
    rows_pad[N // 2 : N // 2 + C, :] = jnp.sum(resid[...], axis=1)
    high, low = split(rows_pad[...])
    ones = jnp.ones((planes, N), BF)
    dims = (((1,), (1,)), ((), ()))
    sums = lax.dot_general(ones, high, dims, preferred_element_type=F32)
    sums = sums + lax.dot_general(ones, low, dims, preferred_element_type=F32)
    for q in range(slab):
        sr[q] = sums
    more = copies(sr, rr, r_send, r_recv, "slab", me, slab)
    launch(more, sr, rr, me)
    finish(pairs)

    y = right3(fx_h[...], fx_l[...], rp[...].reshape(N, N))
    spec[:, :N] = y[:K] + masks[4] * pltpu.roll(y[K:], N // 2, 1)
    spec[:, N:] = jnp.zeros((K, N), F32)

    def expand(row_of, count):
        for p in range(count):
            row, lost = row_of(p)
            row = jnp.broadcast_to(row, (K, N))
            wide[0, p * K : (p + 1) * K, :] = row * masks[1] + jnp.broadcast_to(lost, (K, N)) * masks[5]
            wide[1, p * K : (p + 1) * K, :] = pltpu.roll(row * masks[2], N // 2, 1)
        used = count * K
        s_re[:used, :] = left3(wide[0, :used, :], e_h[...], e_l[...])
        s_im[:used, :] = left3(wide[1, :used, :], e_h[...], e_l[...])

    expand(lambda p: (spec[p : p + 1, :N], spec[p : p + 1, N:]), K)

    @pl.loop(0, K * K // 16)
    def _(block):
        rows = pl.ds(pl.multiple_of(block * 16, 16), 16)
        total_re = jnp.zeros((16, N), F32)
        total_im = jnp.zeros((16, N), F32)
        for t in range(C * C // N):
            lanes = slice(t * N, (t + 1) * N)
            a, b, c, d = s_re[rows, lanes], s_im[rows, lanes], modes[0, rows, lanes], modes[1, rows, lanes]
            total_re += a * c - b * d
            total_im += a * d + b * c
        for part, value in enumerate((total_re, total_im)):
            value = value + pltpu.roll(value, 64, 1)
            mixed[part, rows, :] = value + pltpu.roll(value, 32, 1)

    finish(more)
    sums = jnp.sum(rr[...].reshape(N, N), axis=0, keepdims=True)
    scale = jnp.where(me == 0, 1.0 / (planes * math.sqrt(N * N * N)), 0.0).astype(F32)
    spec[:1, N:] = sums * scale
    high, low = split(jnp.broadcast_to(sums * scale, (K, N)))
    lost = (mm(high, owner[...]) + mm(low, owner[...]))[:1, :]
    for part in range(2):
        value = jnp.zeros((1, N), F32)
        for t in range(C * C // N):
            lanes = slice(t * N, (t + 1) * N)
            value = value + lost[:, lanes] * modes[part, :1, lanes]
        value = value + pltpu.roll(value, 64, 1)
        mixed[part, :1, :] += value + pltpu.roll(value, 32, 1)

    spread = []
    for part in range(2):
        high, low = split(mixed[part])
        spread.append((mm(high, rep[...]) + mm(low, rep[...])))
    for og in range(4):
        lanes = slice(og * N, (og + 1) * N)
        keep = jnp.broadcast_to(masks[0][None], (K, K, N)).reshape(K * K, N)
        re, im = spread[0][:, lanes] * keep, spread[1][:, lanes] * keep
        out_re = right3(ix_h[0], ix_l[0], re) - right3(ix_h[1], ix_l[1], im)
        out_im = right3(ix_h[0], ix_l[0], im) + right3(ix_h[1], ix_l[1], re)
        for h in range(2):
            for d in range(slab):
                first = d * planes + h * some
                sm[h, d, :, 2 * og * N : (2 * og + 1) * N] = out_re[first : first + some]
        for h in range(2):
            for d in range(slab):
                first = d * planes + h * some
                sm[h, d, :, (2 * og + 1) * N : (2 * og + 2) * N] = out_im[first : first + some]

    moving = []
    for h in range(2):
        moving.append(copies(sm.at[h], rm.at[h], m_send.at[h], m_recv.at[h], "slab", me, slab))
        launch(moving[h], sm.at[h], rm.at[h], me)

    @pl.loop(0, planes)
    def _(x):
        @pl.loop(0, C // 4)
        def _(group):
            for chunk in range(4):
                ys = slice(chunk * 32, (chunk + 1) * 32)
                inputs = [prof[i, x, ys, :] for i in range(NIN)]
                for j in range(4):
                    o = group * 4 + j
                    value = mix[0, pl.ds(o, 1), :] * inputs[0] + bias[o]
                    for i in range(1, NIN):
                        value = value + mix[i, pl.ds(o, 1), :] * inputs[i]
                    pre[x, o, ys, :] = value

    c0 = math.sqrt(2.0 / math.pi)
    c1 = c0 * 0.044715

    leaving = []

    def half_planes(h):
        finish(moving[h])
        top = h * some * K
        bottom = top + some * K
        for x in range(some):
            pm[top + x * K : top + (x + 1) * K, :] = rm[h, :, x, :]
        for og in range(4):
            high = pm[top:bottom, og * 2 * N : (og + 1) * 2 * N].astype(BF)
            for t in range(8):
                b_h[og * 8 + t, top:bottom, :] = mm(high, iz[:, t * 2 * N : (t + 1) * 2 * N]).astype(BF)

        @pl.loop(h * some, (h + 1) * some)
        def _(x):
            rows = pl.ds(pl.multiple_of(x * K, K), K)
            acc[...] = jnp.zeros_like(acc)

            def lines(pair):
                blocks = []
                for half in range(2):
                    b = b_h[pair * 2 + half, rows, :]
                    blocks.append(jnp.concatenate([b[:, :N], b[:, N:]], axis=0))
                return mm(iy[...], jnp.concatenate(blocks, axis=1))

            def activate(field, pair):
                w = [[outw[j, pl.ds(pair * 2 + half, 1), :] for j in range(2)] for half in range(2)]
                for chunk in range(4):
                    ys = slice(chunk * 32, (chunk + 1) * 32)
                    add0, add1 = acc[0, ys, :], acc[1, ys, :]
                    for half in range(2):
                        o = pair * 2 + half
                        v = field[ys, half * N : (half + 1) * N] + pre[x, o, ys, :]
                        sq = v * v
                        t = jnp.tanh(v * (c0 + c1 * sq))
                        up = 0.5 + 0.5 * t
                        hidden = (v * up).astype(BF).astype(F32)
                        pre[x, o, ys, :] = up + (0.5 * v) * (1.0 - t * t) * (c0 + (3.0 * c1) * sq)
                        add0 = add0 + w[half][0] * hidden
                        add1 = add1 + w[half][1] * hidden
                    acc[0, ys, :] = add0
                    acc[1, ys, :] = add1

            field_a[...] = lines(0)

            @pl.loop(0, C // 4)
            def _(turn):
                field_b[...] = lines(turn * 2 + 1)
                activate(field_a, turn * 2)
                field_a[...] = lines(jnp.minimum(turn * 2 + 2, C // 2 - 1))
                activate(field_b, turn * 2 + 1)

            for j in range(2):
                value = acc[j] + outb[j]
                pred[j, x] = value
                acc[j] = value - targ[j, x]

            @pl.loop(0, C // 8)
            def _(turn):
                for sub in range(4):
                    pair = turn * 4 + sub
                    parts = []
                    for half in range(2):
                        o = pair * 2 + half
                        grad_o = outw[0, pl.ds(o, 1), :] * acc[0] + outw[1, pl.ds(o, 1), :] * acc[1]
                        parts.append((grad_o * pre[x, o]).astype(BF))
                    u = mm(fy[: 2 * K, :], jnp.concatenate(parts, axis=1))
                    at = pl.multiple_of(pair * 4 * N, 4 * N)
                    for half in range(2):
                        lanes = slice(half * N, (half + 1) * N)
                        ubuf[rows, pl.ds(at + 2 * half * N, N)] = u[:K, lanes]
                        ubuf[rows, pl.ds(at + (2 * half + 1) * N, N)] = u[K:, lanes]

        for og in range(4):
            high, low = split(ubuf[top:bottom, og * 16 * N : (og + 1) * 16 * N])
            v = mm(high, zg[...]) + mm(low, zg[...])
            for x in range(some):
                sg[h, :, x, og * 2 * N : (og + 1) * 2 * N] = v[x * K : (x + 1) * K, :]

        leaving.append(copies(sg.at[h], rg.at[h], g_send.at[h], g_recv.at[h], "slab", me, slab))
        launch(leaving[h], sg.at[h], rg.at[h], me)

    half_planes(0)
    half_planes(1)
    for h in range(2):
        finish(leaving[h])
        for d in range(slab):
            first = d * planes + h * some
            pm[first : first + some, :] = rg[h, d]

    y = right3(fx_h[...], fx_l[...], pm[...])
    for og in range(4):
        re, im = slice(2 * og * N, (2 * og + 1) * N), slice((2 * og + 1) * N, (2 * og + 2) * N)
        out_re = (y[:K, re] - y[K:, im]) * masks[3]
        out_im = (y[:K, im] + y[K:, re]) * masks[3]
        for d in range(dp):
            ps = slice(d * share, (d + 1) * share)
            xs[d, :, re] = out_re[ps]
            xs[d, :, im] = out_im[ps]
    for d in range(dp):
        xs[d, :, 8 * N : 10 * N] = spec[d * share : (d + 1) * share, :]

    pairs = copies(xs, rx, x_send, x_recv, "dp", mine, dp)
    launch(pairs, xs, rx, mine)
    finish(pairs)

    used = share * K
    for d in range(dp):
        expand(lambda p: (rx[d, p : p + 1, 8 * N : 9 * N], rx[d, p : p + 1, 9 * N : 10 * N]), share)
        for part, out in enumerate((g_re, g_im)):
            total = None
            for og in range(4):
                lanes = slice((2 * og + part) * N, (2 * og + part + 1) * N)
                for p in range(share):
                    row = jnp.broadcast_to(rx[d, p : p + 1, lanes], (K, N))
                    wide[0, p * K : (p + 1) * K, :] = row * masks[0]
                high, low = split(wide[0, :used, :])
                term = tile[og * N : (og + 1) * N, :]
                value = mm(high, term) + mm(low, term)
                total = value if total is None else total + value
            out[...] = total
        for t in range(C * C // N):
            lanes = slice(t * N, (t + 1) * N)
            a, b = s_re[:used, lanes], s_im[:used, lanes]
            w_re = a * g_re[...] + b * g_im[...]
            w_im = a * g_im[...] - b * g_re[...]
            if d == 0:
                grad[0, :, lanes] = w_re
                grad[1, :, lanes] = w_im
            else:
                grad[0, :, lanes] += w_re
                grad[1, :, lanes] += w_im


def body(dp, slab, consts, profiles, target_fields, lift_weight, local_weight, local_bias, output_weight, output_bias, mode_weight):
    planes = profiles.shape[2]
    share = K // dp
    vmem = pl.BlockSpec(memory_space=pltpu.VMEM)
    smem = pl.BlockSpec(memory_space=pltpu.SMEM)
    dma = pltpu.SemaphoreType.DMA
    pred, grad = pl.pallas_call(
        functools.partial(kernel, dp, slab),
        out_shape=(jax.ShapeDtypeStruct((2, planes, N, N), F32), jax.ShapeDtypeStruct((2, share * K, C * C), F32)),
        in_specs=[vmem] * 6 + [smem] * 3 + [vmem] * len(consts),
        out_specs=(vmem, vmem),
        scratch_shapes=[
            pltpu.VMEM((planes * K, C * 2 * N), F32),
            pltpu.VMEM((C, 8, N), F32),
            pltpu.VMEM((N, N), F32),
            pltpu.VMEM((slab, planes, N), F32),
            pltpu.VMEM((slab, planes, N), F32),
            pltpu.VMEM((slab, planes, N), F32),
            pltpu.VMEM((slab, planes, N), F32),
            pltpu.VMEM((K, 2 * N), F32),
            pltpu.VMEM((N, C * C), BF),
            pltpu.VMEM((N, C * C), BF),
            pltpu.VMEM((2, K * K, N), F32),
            pltpu.VMEM((K * K, C * C), F32),
            pltpu.VMEM((K * K, C * C), F32),
            pltpu.VMEM((2, K * K, N), F32),
            pltpu.VMEM((2, slab, planes // 2, 8 * N), F32),
            pltpu.VMEM((2, slab, planes // 2, 8 * N), F32),
            pltpu.VMEM((planes * K, 8 * N), F32),
            pltpu.VMEM((C, planes * K, 2 * N), BF),
            pltpu.VMEM((N, 2 * N), F32),
            pltpu.VMEM((N, 2 * N), F32),
            pltpu.VMEM((planes, C, N, N), F32),
            pltpu.VMEM((NIN, C, N), F32),
            pltpu.VMEM((2, C, N), F32),
            pltpu.VMEM((2, N, N), F32),
            pltpu.VMEM((2, slab, planes // 2, 8 * N), F32),
            pltpu.VMEM((2, slab, planes // 2, 8 * N), F32),
            pltpu.VMEM((dp, share, 10 * N), F32),
            pltpu.VMEM((dp, share, 10 * N), F32),
            pltpu.VMEM((share * K, N), F32),
            pltpu.VMEM((share * K, N), F32),
            dma((slab,)), dma((slab,)), dma((slab,)), dma((slab,)),
            dma((2, slab)), dma((2, slab)), dma((2, slab)), dma((2, slab)), dma((dp,)), dma((dp,)),
        ],
        compiler_params=pltpu.CompilerParams(collective_id=0, has_side_effects=True, vmem_limit_bytes=56 << 20),
    )(profiles[0], target_fields[0], mode_weight.reshape(2, K * K, C * C), lift_weight, local_weight,
      output_weight.T, lift_weight, local_bias, output_bias, *consts)
    return pred[None], grad.reshape(2, 1, share, K, C * C)


def solution(mesh):
    consts = tables()
    in_specs = (
        P("dp", None, "slab", None, None),
        P("dp", None, "slab", None, None),
        P(),
        P(),
        P(),
        P(),
        P(),
        P(None, "slab", None, None, None),
    )
    out_specs = (P("dp", None, "slab", None, None), P(None, "slab", "dp", None, None))

    def run(*args):
        return body(mesh.shape["dp"], mesh.shape["slab"], [jnp.asarray(c) for c in consts], *args)

    return jax.shard_map(run, mesh=mesh, in_specs=in_specs, out_specs=out_specs, check_vma=False)
```
